128 devices in a mesh: row: 8 (over z, core), col: 16 (over y, x).
Axes of the slice: x: 4, y: 4, z: 4, core: 2. Of those that a mesh axis runs over, the one named last changes fastest.
Arguments:
- lam_tiles: bfloat16 [128, 128, 16, 128], P(('row', 'col')), may hold values from -6 to 6
- lam_ids: int32 [128, 128], P(('row', 'col')), may hold values from 0 to 511, as said below
- integrals: bfloat16 [8192, 65536], P('row', 'col'), may hold values from -0.09375 to 0.09375
Outputs:
- ladder: float32 [2048, 8192], P('col', 'row')
The draws below stay inside these ranges and needn't reach their ends.
Inputs may be any that keep to these rules, and one draw needn't show every extreme that they name: `lam_ids`: within a group the 128 ids are distinct; at most 16 of them lie in one block of 32 consecutive ids, and every group has exactly 16 in one block, the same block for all groups.
All inputs are finite; a program needn't handle non-finite values.
Results may differ from the reference program's by a relative error of at most 0.0003.
Values may be sent and summed in bfloat16 or wider, within the bound.
A program may use at most 128 MiB of HBM per device.

```python
import jax
import jax.numpy as jnp
from jax import lax

TILE = 128
PG = 16
KT_DEV = 32
CAP = 16
G = 128
S = 128
KT = 512
NAB = 8192


def draw_lam_ids(key, part):
    blocks = KT // KT_DEV
    key_hot, key_bias, key_noise, key_perm = jax.random.split(key, 4)
    hot = jax.random.randint(key_hot, (), 0, blocks)
    bias = jax.random.randint(key_bias, (blocks,), 0, 65536)
    bias = jnp.where(jnp.arange(blocks) == hot, 4194304, bias)
    noise = jax.random.randint(key_noise, (G, blocks, CAP), 0, 65536)
    score = (bias[None, :, None] + noise).reshape(G, blocks * CAP)
    score = score * (blocks * CAP) + jnp.arange(blocks * CAP, dtype=jnp.int32)[None, :]
    chosen = lax.top_k(score, S)[1].astype(jnp.int32)
    block = chosen // CAP
    slot = chosen % CAP
    ranks = jax.random.randint(key_perm, (G, blocks, KT_DEV), 0, 1048576) * KT_DEV + jnp.arange(KT_DEV, dtype=jnp.int32)
    order = jnp.argsort(ranks, axis=-1).astype(jnp.int32).reshape(G, blocks * KT_DEV)
    within = jnp.take_along_axis(order, block * KT_DEV + slot, axis=1)
    return (block * KT_DEV + within).astype(jnp.int32)


def steps_of(rng, shape, pieces, least, largest):
    loudness = 1.0
    for axis_at, blocks in pieces:
        draws = jax.random.uniform(jax.random.fold_in(jax.random.fold_in(rng, 6), axis_at), (blocks,), jnp.float32, least / len(pieces), largest / len(pieces))
        loudness = loudness * jnp.repeat(jnp.exp(draws), shape[axis_at] // blocks).reshape((-1,) + (1,) * (len(shape) - 1 - axis_at))
    return loudness


def gaussian(key, dims, deviation, reach, shards=(), kind=jnp.bfloat16):
    loudness = steps_of(key, dims, shards, -0.22, 0.18) if shards else 1.0
    entries = jax.random.normal(key, dims, jnp.float32) * deviation * loudness
    return jnp.minimum(jnp.maximum(entries, -reach), reach).astype(kind)


def setup_inputs(seed: int = 0) -> dict:
    splits = jax.random.split(jax.random.key(seed), 4)
    lam_tiles = gaussian(splits[0], (G, S, PG, TILE), 1.0, 6.0, ((0, 128),))
    lam_ids = draw_lam_ids(jax.random.fold_in(splits[3], 71), 0)
    integrals = gaussian(splits[2], (NAB, KT * TILE), (S * TILE // 4) ** -0.5, 0.09375, ((0, 8), (1, 16)))
    return {"lam_tiles": lam_tiles, "lam_ids": lam_ids, "integrals": integrals}


def reference(lam_tiles, lam_ids, integrals):
    columns = integrals.reshape(integrals.shape[0], KT, TILE)

    def one_group(group_args):
        tiles, ids = group_args
        picked = jnp.take(columns, ids.astype(jnp.int32), axis=1)
        flat_cols = picked.reshape(picked.shape[0], S * TILE)
        flat_tiles = jnp.transpose(tiles, (1, 0, 2)).reshape(PG, S * TILE)
        product = lax.dot_general(flat_tiles, flat_cols, (((1,), (1,)), ((), ())), preferred_element_type=jnp.float32)
        return 0.5 * product

    result = lax.map(one_group, (lam_tiles, lam_ids))
    return result.reshape(G * PG, NAB)
```

```python
import functools

import jax
import jax.numpy as jnp
from jax import lax
from jax.experimental import pallas as pl
from jax.experimental.pallas import tpu as pltpu
from jax.sharding import PartitionSpec as P

CAP = 16
MESH = pl.DeviceIdType.MESH
DYS = (0, 1, 3, 2)
NT = (((1,), (1,)), ((), ()))
OWN, PART, ZM, ZP, PZM, PZP, Z2, PZ2 = range(8)
STEPS = (OWN, PART, ZM, ZP, PZM, PZP, Z2, PZ2)
OFFSET = {OWN: 0, PART: 0, ZM: 3, PZM: 3, ZP: 1, PZP: 1, Z2: 2, PZ2: 2}


def bucket_kernel(place_ref, lam_ref, out_ref):
    def body(s, carry):
        out_ref[place_ref[s]] = lam_ref[s]
        return carry

    lax.fori_loop(0, lam_ref.shape[0], body, 0, unroll=8)


def bucket(place, tiles, slots):
    return pl.pallas_call(
        bucket_kernel,
        out_shape=jax.ShapeDtypeStruct((slots,) + tiles.shape[1:], tiles.dtype),
        in_specs=[
            pl.BlockSpec(memory_space=pltpu.SMEM),
            pl.BlockSpec(memory_space=pltpu.VMEM),
        ],
        out_specs=pl.BlockSpec(memory_space=pltpu.VMEM),
        name="bucket",
    )(place, tiles)


def wide(scale, width):
    return jnp.concatenate([jnp.concatenate([scale, scale], axis=0)] * (width // 128), axis=1)


def quantize(src, dst, scale_dst):
    rows, width = src.shape

    def largest(r, m):
        a = jnp.abs(src[pl.ds(r * 16, 16), :])
        for j in range(width // 128):
            part = a[:, j * 128 : (j + 1) * 128]
            m = jnp.maximum(m, jnp.maximum(part[:8], part[8:]))
        return m

    m = lax.fori_loop(0, rows // 16, largest, jnp.zeros((8, 128), jnp.float32), unroll=2)
    scale_dst[...] = m * (1.0 / 32767.0)
    inverse = wide(jnp.where(m > 0.0, 32767.0 / m, 0.0), width)

    def code(r, carry):
        at = pl.ds(pl.multiple_of(r * 16, 16), 16)
        dst[at, :] = jnp.round(src[at, :] * inverse).astype(jnp.int32).astype(jnp.int16)
        return carry

    lax.fori_loop(0, rows // 16, code, 0, unroll=2)


def add_coded(acc, coded, scales, factor=None, out=None):
    rows, width = acc.shape
    w = [wide(scales[j], width) for j in range(3)]

    def body(r, carry):
        at = pl.ds(pl.multiple_of(r * 16, 16), 16)
        total = acc[at, :]
        for j in range(3):
            total = total + coded[j, at, :].astype(jnp.int32).astype(jnp.float32) * w[j]
        if out is None:
            acc[at, :] = total
        else:
            out[at, :] = factor * total
        return carry

    lax.fori_loop(0, rows // 16, body, 0, unroll=2)


def ladder_kernel(
    buf_ref, inv_ref, int_ref, out_ref,
    r0, r1, r2, r3, r4, r5, r6, r7, tabs, smem, ints, dense, prod,
    q1, s1, q2, s2, q3, s3, q4, s4,
    rq1, rs1, rq2, rs2, rq3, rs3, rq4, rs4,
    acc1, acc2, fin1, fin2,
    int_sem, smem_sem, loc_sem,
    ta_send, ta_recv, t_send, t_recv,
    a_send, a_recv, b_send, b_recv, c_send, c_recv, d_send, d_recv,
    q1_send, q1_recv, q2_send, q2_recv, q3_send, q3_recv, q4_send, q4_recv,
    s1_send, s1_recv, s2_send, s2_recv, s3_send, s3_recv, s4_send, s4_recv,
):
    rbuf = (r0, r1, r2, r3, r4, r5, r6, r7)
    row, col = lax.axis_index("row"), lax.axis_index("col")
    z, core = row // 2, row % 2
    y, x = col // 4, col % 4
    up = ((z + 1) % 4) * 2 + core
    down = ((z + 3) % 4) * 2 + core
    partner = z * 2 + (1 - core)

    barrier = pltpu.get_barrier_semaphore()

    def greet(j, carry):
        pl.semaphore_signal(barrier, inc=1, device_id={"row": row, "col": (col + j) % 16}, device_id_type=MESH)
        return carry

    lax.fori_loop(1, 16, greet, 0)
    for other in (up, down, partner):
        pl.semaphore_signal(barrier, inc=1, device_id={"row": other, "col": col}, device_id_type=MESH)
    pl.semaphore_wait(barrier, 18)

    def remote(src, dst, send, recv, to_row, to_col):
        return pltpu.make_async_remote_copy(
            src_ref=src, dst_ref=dst, send_sem=send, recv_sem=recv,
            device_id={"row": to_row, "col": to_col}, device_id_type=MESH,
        )

    def wait_bytes(ref, sem):
        pltpu.make_async_copy(ref, ref, sem).wait()

    load = pltpu.make_async_copy(int_ref, ints, int_sem)

    mine = pl.ds(col, 1)
    own_table = pltpu.make_async_copy(inv_ref.at[mine], tabs.at[OWN, mine], ta_recv)
    own_table.start()

    def send_table(j, carry):
        to = (col + j) % 16
        remote(inv_ref.at[pl.ds(to, 1)], tabs.at[OWN, mine], ta_send.at[j], ta_recv, row, to).start()
        return carry

    lax.fori_loop(1, 16, send_table, 0)

    here = pl.ds(pl.multiple_of(col * CAP, CAP), CAP)
    pltpu.make_async_copy(buf_ref.at[here], r0.at[here], a_recv.at[0]).start()

    def tile_copy(dy, j):
        to = ((y + 4 - dy) % 4) * 4 + (x + j) % 4
        there = pl.ds(pl.multiple_of(to * CAP, CAP), CAP)
        return remote(buf_ref.at[there], r0.at[here], a_send.at[dy * 4 + j], a_recv.at[dy], row, to)

    for dy in DYS:
        for j in range(1 if dy == 0 else 0, 4):
            tile_copy(dy, j).start()
    load.start()

    zero = jnp.zeros((16, 128), jnp.bfloat16)
    for r in rbuf:
        r[16 * CAP] = zero

    wait_bytes(tabs.at[OWN], ta_recv)
    t_own = [
        remote(tabs.at[OWN], tabs.at[ZM], t_send.at[0], t_recv.at[ZM], up, col),
        remote(tabs.at[OWN], tabs.at[ZP], t_send.at[1], t_recv.at[ZP], down, col),
        remote(tabs.at[OWN], tabs.at[PART], t_send.at[2], t_recv.at[PART], partner, col),
    ]
    for t in t_own:
        t.start()

    def quarter(dy):
        return pl.ds(pl.multiple_of(((y + dy) % 4) * 4 * CAP, 4 * CAP), 4 * CAP)

    def b_copies(dy):
        at = quarter(dy)
        return [
            remote(r0.at[at], rbuf[ZM].at[at], b_send.at[0, dy], b_recv.at[0, dy], up, col),
            remote(r0.at[at], rbuf[ZP].at[at], b_send.at[1, dy], b_recv.at[1, dy], down, col),
            remote(r0.at[at], rbuf[PART].at[at], b_send.at[2, dy], b_recv.at[2, dy], partner, col),
        ]

    def c_copy(dy):
        at = quarter(dy)
        if dy in (0, 3):
            return remote(rbuf[ZP].at[at], rbuf[Z2].at[at], c_send.at[dy], c_recv.at[dy], down, col)
        return remote(rbuf[ZM].at[at], rbuf[Z2].at[at], c_send.at[dy], c_recv.at[dy], up, col)

    def d_copy(which, dy):
        at = quarter(dy)
        src, dst = ((ZM, PZM), (ZP, PZP), (Z2, PZ2))[which]
        return remote(rbuf[src].at[at], rbuf[dst].at[at], d_send.at[which, dy], d_recv.at[which, dy], partner, col)

    for dy in DYS:
        wait_bytes(r0.at[quarter(dy)], a_recv.at[dy])
        for copy in b_copies(dy):
            copy.start()

    def arrived(buf, sem, dys=DYS):
        for dy in dys:
            wait_bytes(rbuf[buf].at[quarter(dy)], sem.at[dy])

    def where_from(step):
        zi = (z + OFFSET[step]) % 4
        ki = core if step in (OWN, ZM, ZP, Z2) else 1 - core
        return zi, ki

    def compute(step):
        fetch = pltpu.make_async_copy(tabs.at[step], smem, smem_sem)
        fetch.start()
        fetch.wait()
        tiles = rbuf[step]

        def build(g, carry):
            for k in range(32):
                dense[pl.ds(pl.multiple_of(g * 16, 16), 16), k * 128 : (k + 1) * 128] = tiles[smem[g, 0, k]]
            return carry

        lax.fori_loop(0, 16, build, 0)

        def columns(n, carry):
            at = pl.ds(pl.multiple_of(n * 256, 256), 256)
            prod[:, at] = lax.dot_general(dense[...], ints[at, :], NT, preferred_element_type=jnp.float32)
            return carry

        lax.fori_loop(0, 4, columns, 0)

    def q1_copies(step):
        zi, ki = where_from(step)
        d = (y + 3 - zi) % 4
        to = zi * 4 + x
        return (
            remote(q1.at[step], rq1.at[ki, d], q1_send.at[step], q1_recv.at[ki, d], row, to),
            remote(s1.at[step], rs1.at[ki, d], s1_send.at[step], s1_recv.at[ki, d], row, to),
        )

    def q2_copies(step, e):
        zi, ki = where_from(step)
        xd = 2 * ki + e
        d = (x + 3 - xd) % 4
        to = y * 4 + xd
        return (
            remote(q2.at[step, e], rq2.at[zi, d], q2_send.at[step, e], q2_recv.at[zi, d], row, to),
            remote(s2.at[step, e], rs2.at[zi, d], s2_send.at[step, e], s2_recv.at[zi, d], row, to),
        )

    def q3_copies(step, e):
        zi, ki = where_from(step)
        xd = 2 * ki + e
        d = (x + 3 - xd) % 4
        to = zi * 4 + xd
        return (
            remote(q3.at[ki, e], rq3.at[d], q3_send.at[ki, e], q3_recv.at[d], row, to),
            remote(s3.at[ki, e], rs3.at[d], s3_send.at[ki, e], s3_recv.at[d], row, to),
        )

    def q4_copies(step):
        zi, ki = where_from(step)
        d = (y + 3 - zi) % 4
        to = zi * 4 + x
        return (
            remote(q4.at[zi], rq4.at[d], q4_send.at[zi], q4_recv.at[d], row, to),
            remote(s4.at[zi], rs4.at[d], s4_send.at[zi], s4_recv.at[d], row, to),
        )

    def move(src, dst):
        rows = src.shape[0]

        def body(r, carry):
            at = pl.ds(pl.multiple_of(r * 16, 16), 16)
            dst[at, :] = src[at, :]
            return carry

        lax.fori_loop(0, rows // 16, body, 0)

    def first_sends(step):
        zi, ki = where_from(step)
        left, right = prod.at[:, pl.ds(0, 512)], prod.at[:, pl.ds(512, 512)]

        @pl.when(y != zi)
        def _():
            quantize(left, q1.at[step], s1.at[step])
            for copy in q1_copies(step):
                copy.start()

        @pl.when(y == zi)
        def _():
            move(left, acc1.at[ki])

        for e in range(2):
            part = right.at[pl.ds(e * 128, 128), :]

            @pl.when(x != 2 * ki + e)
            def _():
                quantize(part, q2.at[step, e], s2.at[step, e])
                for copy in q2_copies(step, e):
                    copy.start()

            @pl.when(x == 2 * ki + e)
            def _():
                move(part, acc2.at[zi])

    def second_sends(step):
        zi, ki = where_from(step)

        @pl.when(y == zi)
        def _():
            for d in range(3):
                wait_bytes(rq1.at[ki, d], q1_recv.at[ki, d])
                wait_bytes(rs1.at[ki, d], s1_recv.at[ki, d])
            add_coded(acc1.at[ki], rq1.at[ki], rs1.at[ki])
            for e in range(2):
                part = acc1.at[ki, pl.ds(e * 128, 128), :]

                @pl.when(x != 2 * ki + e)
                def _():
                    quantize(part, q3.at[ki, e], s3.at[ki, e])
                    for copy in q3_copies(step, e):
                        copy.start()

                @pl.when(x == 2 * ki + e)
                def _():
                    move(part, fin1)

        @pl.when(x // 2 == ki)
        def _():
            for d in range(3):
                wait_bytes(rq2.at[zi, d], q2_recv.at[zi, d])
                wait_bytes(rs2.at[zi, d], s2_recv.at[zi, d])
            add_coded(acc2.at[zi], rq2.at[zi], rs2.at[zi])

            @pl.when(y != zi)
            def _():
                quantize(acc2.at[zi], q4.at[zi], s4.at[zi])
                for copy in q4_copies(step):
                    copy.start()

            @pl.when(y == zi)
            def _():
                move(acc2.at[zi], fin2)

    load.wait()
    compute(OWN)
    first_sends(OWN)

    wait_bytes(tabs.at[ZM], t_recv.at[ZM])
    wait_bytes(tabs.at[ZP], t_recv.at[ZP])
    t_more = [
        remote(tabs.at[ZP], tabs.at[Z2], t_send.at[3], t_recv.at[Z2], down, col),
        remote(tabs.at[ZM], tabs.at[PZM], t_send.at[4], t_recv.at[PZM], partner, col),
        remote(tabs.at[ZP], tabs.at[PZP], t_send.at[5], t_recv.at[PZP], partner, col),
    ]
    for t in t_more:
        t.start()

    def pass_on(dys):
        for dy in dys:
            wait_bytes(rbuf[ZM].at[quarter(dy)], b_recv.at[0, dy])
            wait_bytes(rbuf[ZP].at[quarter(dy)], b_recv.at[1, dy])
            c_copy(dy).start()
            d_copy(0, dy).start()
            d_copy(1, dy).start()

    pass_on(DYS[:2])
    wait_bytes(tabs.at[PART], t_recv.at[PART])
    arrived(PART, b_recv.at[2])
    compute(PART)
    first_sends(PART)
    second_sends(OWN)
    pass_on(DYS[2:])

    compute(ZM)
    first_sends(ZM)
    second_sends(PART)

    wait_bytes(tabs.at[Z2], t_recv.at[Z2])
    t_last = remote(tabs.at[Z2], tabs.at[PZ2], t_send.at[6], t_recv.at[PZ2], partner, col)
    t_last.start()

    compute(ZP)
    first_sends(ZP)
    second_sends(ZM)

    def pass_far(dys):
        for dy in dys:
            wait_bytes(rbuf[Z2].at[quarter(dy)], c_recv.at[dy])
            d_copy(2, dy).start()

    wait_bytes(tabs.at[PZM], t_recv.at[PZM])
    arrived(PZM, d_recv.at[0])
    compute(PZM)
    first_sends(PZM)
    second_sends(ZP)
    pass_far(DYS[:2])

    wait_bytes(tabs.at[PZP], t_recv.at[PZP])
    arrived(PZP, d_recv.at[1])
    compute(PZP)
    first_sends(PZP)
    second_sends(PZM)
    pass_far(DYS[2:])

    compute(Z2)
    first_sends(Z2)
    second_sends(PZP)

    wait_bytes(tabs.at[PZ2], t_recv.at[PZ2])
    arrived(PZ2, d_recv.at[2])
    compute(PZ2)
    first_sends(PZ2)
    second_sends(Z2)
    second_sends(PZ2)

    for d in range(3):
        wait_bytes(rq3.at[d], q3_recv.at[d])
        wait_bytes(rs3.at[d], s3_recv.at[d])
    add_coded(fin1, rq3, rs3, 0.5, out_ref.at[:, pl.ds(0, 512)])
    for d in range(3):
        wait_bytes(rq4.at[d], q4_recv.at[d])
        wait_bytes(rs4.at[d], s4_recv.at[d])
    add_coded(fin2, rq4, rs4, 0.5, out_ref.at[:, pl.ds(512, 512)])

    def table_left(j, carry):
        remote(inv_ref.at[mine], tabs.at[OWN, mine], ta_send.at[j], ta_recv, row, (col + j) % 16).wait_send()
        return carry

    lax.fori_loop(1, 16, table_left, 0)
    for t in t_own + t_more + [t_last]:
        t.wait_send()
    for dy in DYS:
        for j in range(1 if dy == 0 else 0, 4):
            tile_copy(dy, j).wait_send()
        for copy in b_copies(dy):
            copy.wait_send()
        c_copy(dy).wait_send()
        for which in range(3):
            d_copy(which, dy).wait_send()
    for step in STEPS:
        zi, ki = where_from(step)

        @pl.when(y != zi)
        def _():
            for copy in q1_copies(step):
                copy.wait_send()

        for e in range(2):

            @pl.when(x != 2 * ki + e)
            def _():
                for copy in q2_copies(step, e):
                    copy.wait_send()

            @pl.when((y == zi) & (x != 2 * ki + e))
            def _():
                for copy in q3_copies(step, e):
                    copy.wait_send()

        @pl.when((y != zi) & (x // 2 == ki))
        def _():
            for copy in q4_copies(step):
                copy.wait_send()


def ladder(buf, inv, integrals):
    ab, cd = integrals.shape
    half = ab // 2
    i16, f32, bf16 = jnp.int16, jnp.float32, jnp.bfloat16
    dma = pltpu.SemaphoreType.DMA
    vmem = pltpu.VMEM
    scratch = [vmem((16 * CAP + 1, 16, 128), bf16) for _ in range(8)]
    scratch += [
        vmem((8, 16, 1, 128), jnp.int32), pltpu.SMEM((16, 1, 128), jnp.int32),
        vmem((ab, cd), bf16), vmem((256, cd), bf16), vmem((256, ab), f32),
        vmem((8, 256, half), i16), vmem((8, 8, 128), f32),
        vmem((8, 2, 128, half), i16), vmem((8, 2, 8, 128), f32),
        vmem((2, 2, 128, half), i16), vmem((2, 2, 8, 128), f32),
        vmem((4, 128, half), i16), vmem((4, 8, 128), f32),
        vmem((2, 3, 256, half), i16), vmem((2, 3, 8, 128), f32),
        vmem((4, 3, 128, half), i16), vmem((4, 3, 8, 128), f32),
        vmem((3, 128, half), i16), vmem((3, 8, 128), f32),
        vmem((3, 128, half), i16), vmem((3, 8, 128), f32),
        vmem((2, 256, half), f32), vmem((4, 128, half), f32),
        vmem((128, half), f32), vmem((128, half), f32),
        dma, dma, dma,
        dma((16,)), dma, dma((7,)), dma((8,)),
        dma((16,)), dma((4,)), dma((3, 4)), dma((3, 4)), dma((4,)), dma((4,)), dma((3, 4)), dma((3, 4)),
        dma((8,)), dma((2, 3)), dma((8, 2)), dma((4, 3)), dma((2, 2)), dma((3,)), dma((4,)), dma((3,)),
        dma((8,)), dma((2, 3)), dma((8, 2)), dma((4, 3)), dma((2, 2)), dma((3,)), dma((4,)), dma((3,)),
    ]
    any_space = pl.BlockSpec(memory_space=pl.ANY)
    return pl.pallas_call(
        ladder_kernel,
        out_shape=jax.ShapeDtypeStruct((128, ab), f32),
        in_specs=[any_space, any_space, any_space],
        out_specs=pl.BlockSpec(memory_space=pltpu.VMEM),
        scratch_shapes=scratch,
        compiler_params=pltpu.CompilerParams(collective_id=0, has_side_effects=True, vmem_limit_bytes=60 << 20),
        name="ladder",
    )(buf, inv, integrals)


def tables(ids, col, n_col, kt_dev):
    block = ids // kt_dev
    lower = (block[:, None] == block[None, :]) & (ids[None, :] < ids[:, None])
    place = block * CAP + jnp.sum(lower.astype(jnp.int32), axis=1)
    tile = jnp.arange(n_col * kt_dev, dtype=jnp.int32)
    present = jnp.any(ids[None, :] == tile[:, None], axis=1)
    before = (block[None, :] == (tile // kt_dev)[:, None]) & (ids[None, :] < tile[:, None])
    rank = jnp.sum(before.astype(jnp.int32), axis=1)
    inv = jnp.where(present, col * CAP + rank, n_col * CAP).reshape(n_col, 1, kt_dev)
    return place, jnp.pad(inv, ((0, 0), (0, 0), (0, 128 - kt_dev)))


def shards(lam_tiles, lam_ids, integrals):
    n_col = lax.axis_size("col")
    _, s_count, pairs, tile = lam_tiles.shape
    kt_dev = integrals.shape[1] // tile
    place, inv = tables(lam_ids.reshape(-1), lax.axis_index("col"), n_col, kt_dev)
    buf = bucket(place, lam_tiles.reshape(s_count, pairs, tile), n_col * CAP)
    return ladder(buf, inv, integrals)


def solution(mesh):
    return jax.shard_map(
        shards,
        mesh=mesh,
        in_specs=(P(("row", "col"), None, None, None), P(("row", "col"), None), P("row", "col")),
        out_specs=P("col", "row"),
        check_vma=False,
    )
```

```python
import functools

import jax
import jax.numpy as jnp
from jax import lax
from jax.experimental import pallas as pl
from jax.experimental.pallas import tpu as pltpu
from jax.sharding import PartitionSpec as P

CAP = 16
MESH = pl.DeviceIdType.MESH
DYS = (0, 1, 3, 2)
NT = (((1,), (1,)), ((), ()))
OWN, PART, ZM, ZP, PZM, PZP, Z2, PZ2 = range(8)
STEPS = (OWN, PART, ZM, ZP, PZM, PZP, Z2, PZ2)
OFFSET = {OWN: 0, PART: 0, ZM: 3, PZM: 3, ZP: 1, PZP: 1, Z2: 2, PZ2: 2}


def bucket_kernel(ids_ref, lam_ref, out_ref, inv_ref, used):
    n_col, _, _ = inv_ref.shape
    kt = 32
    first = lax.axis_index("col") * CAP

    def clear(b, carry):
        used[b] = 0
        for k in range(kt):
            inv_ref[b, 0, k] = n_col * CAP
        return carry

    lax.fori_loop(0, n_col, clear, 0)

    def body(s, carry):
        tile = ids_ref[0, s]
        b = tile // kt
        slot = used[b]
        used[b] = slot + 1
        inv_ref[b, 0, tile % kt] = first + slot
        out_ref[b * CAP + slot] = lam_ref[s]
        return carry

    lax.fori_loop(0, lam_ref.shape[0], body, 0, unroll=8)


def bucket(ids, tiles, n_col):
    return pl.pallas_call(
        bucket_kernel,
        out_shape=(
            jax.ShapeDtypeStruct((n_col * CAP,) + tiles.shape[1:], tiles.dtype),
            jax.ShapeDtypeStruct((n_col, 1, 128), jnp.int32),
        ),
        in_specs=[
            pl.BlockSpec(memory_space=pltpu.SMEM),
            pl.BlockSpec(memory_space=pltpu.VMEM),
        ],
        out_specs=(
            pl.BlockSpec(memory_space=pltpu.VMEM),
            pl.BlockSpec(memory_space=pltpu.SMEM),
        ),
        scratch_shapes=[pltpu.SMEM((n_col,), jnp.int32)],
        name="bucket",
    )(ids, tiles)


def wide(scale, width):
    return jnp.concatenate([jnp.concatenate([scale, scale], axis=0)] * (width // 128), axis=1)


def quantize(src, dst, scale_dst):
    rows, width = src.shape

    def largest(r, m):
        a = jnp.abs(src[pl.ds(r * 16, 16), :])
        for j in range(width // 128):
            part = a[:, j * 128 : (j + 1) * 128]
            m = jnp.maximum(m, jnp.maximum(part[:8], part[8:]))
        return m

    m = lax.fori_loop(0, rows // 16, largest, jnp.zeros((8, 128), jnp.float32), unroll=2)
    scale_dst[...] = m * (1.0 / 32767.0)
    inverse = wide(jnp.where(m > 0.0, 32767.0 / m, 0.0), width)

    def code(r, carry):
        at = pl.ds(pl.multiple_of(r * 16, 16), 16)
        dst[at, :] = jnp.round(src[at, :] * inverse).astype(jnp.int32).astype(jnp.int16)
        return carry

    lax.fori_loop(0, rows // 16, code, 0, unroll=2)


def add_coded(acc, coded, scales, factor=None, out=None):
    rows, width = acc.shape
    w = [wide(scales[j], width) for j in range(3)]

    def body(r, carry):
        at = pl.ds(pl.multiple_of(r * 16, 16), 16)
        total = acc[at, :]
        for j in range(3):
            total = total + coded[j, at, :].astype(jnp.int32).astype(jnp.float32) * w[j]
        if out is None:
            acc[at, :] = total
        else:
            out[at, :] = factor * total
        return carry

    lax.fori_loop(0, rows // 16, body, 0, unroll=2)


def ladder_kernel(
    buf_ref, inv_ref, int_ref, out_ref,
    r0, r1, r2, r3, r4, r5, r6, r7, tabs, smem, ints, dense0, dense1, prod,
    q1, s1, q2, s2, q3, s3, q4, s4,
    rq1, rs1, rq2, rs2, rq3, rs3, rq4, rs4,
    q5, s5, rq5, rs5, acc5, q6, s6,
    acc1, acc2, fin1, fin2,
    int_sem, smem_sem, loc_sem,
    ta_send, ta_recv, t_send, t_recv,
    a_send, a_recv, b_send, b_recv, c_send, c_recv, d_send, d_recv,
    q1_send, q1_recv, q2_send, q2_recv, q3_send, q3_recv, q4_send, q4_recv,
    e_recv, e_send, q5_send, q5_recv, s5_send, s5_recv, q6_send, s6_send,
    s1_send, s1_recv, s2_send, s2_recv, s3_send, s3_recv, s4_send, s4_recv,
):
    dense = (dense0, dense1)
    rbuf = (r0, r1, r2, r3, r4, r5, r6, r7)
    row, col = lax.axis_index("row"), lax.axis_index("col")
    z, core = row // 2, row % 2
    y, x = col // 4, col % 4
    up = ((z + 1) % 4) * 2 + core
    down = ((z + 3) % 4) * 2 + core
    partner = z * 2 + (1 - core)

    barrier = pltpu.get_barrier_semaphore()

    def greet(j, carry):
        pl.semaphore_signal(barrier, inc=1, device_id={"row": row, "col": (col + j) % 16}, device_id_type=MESH)
        return carry

    lax.fori_loop(1, 16, greet, 0)
    for other in (up, down, partner):
        pl.semaphore_signal(barrier, inc=1, device_id={"row": other, "col": col}, device_id_type=MESH)
    pl.semaphore_wait(barrier, 18)

    def remote(src, dst, send, recv, to_row, to_col):
        return pltpu.make_async_remote_copy(
            src_ref=src, dst_ref=dst, send_sem=send, recv_sem=recv,
            device_id={"row": to_row, "col": to_col}, device_id_type=MESH,
        )

    def wait_bytes(ref, sem):
        pltpu.make_async_copy(ref, ref, sem).wait()

    load = pltpu.make_async_copy(int_ref, ints, int_sem)

    mine = pl.ds(col, 1)
    own_table = pltpu.make_async_copy(inv_ref.at[mine], tabs.at[OWN, mine], ta_recv)
    own_table.start()

    def send_table(j, carry):
        to = (col + j) % 16
        remote(inv_ref.at[pl.ds(to, 1)], tabs.at[OWN, mine], ta_send.at[j], ta_recv, row, to).start()
        return carry

    lax.fori_loop(1, 16, send_table, 0)

    here = pl.ds(pl.multiple_of(col * CAP, CAP), CAP)
    pltpu.make_async_copy(buf_ref.at[here], r0.at[here], e_recv.at[0]).start()

    def tile_copy(dy, j):
        to = ((y + 4 - dy) % 4) * 4 + (x + j) % 4
        there = pl.ds(pl.multiple_of(to * CAP, CAP), CAP)
        arrival = e_recv.at[j] if dy == 0 else a_recv.at[dy]
        return remote(buf_ref.at[there], r0.at[here], a_send.at[dy * 4 + j], arrival, row, to)

    for dy in DYS:
        for j in range(1 if dy == 0 else 0, 4):
            tile_copy(dy, j).start()
    load.start()

    zero = jnp.zeros((16, 128), jnp.bfloat16)
    for r in rbuf:
        r[16 * CAP] = zero

    t_own = [
        remote(tabs.at[OWN], tabs.at[ZM], t_send.at[0], t_recv.at[ZM], up, col),
        remote(tabs.at[OWN], tabs.at[ZP], t_send.at[1], t_recv.at[ZP], down, col),
        remote(tabs.at[OWN], tabs.at[PART], t_send.at[2], t_recv.at[PART], partner, col),
    ]

    def quarter(dy):
        return pl.ds(pl.multiple_of(((y + dy) % 4) * 4 * CAP, 4 * CAP), 4 * CAP)

    def b_copies(dy):
        at = quarter(dy)
        return [
            remote(r0.at[at], rbuf[ZM].at[at], b_send.at[0, dy], b_recv.at[0, dy], up, col),
            remote(r0.at[at], rbuf[ZP].at[at], b_send.at[1, dy], b_recv.at[1, dy], down, col),
            remote(r0.at[at], rbuf[PART].at[at], b_send.at[2, dy], b_recv.at[2, dy], partner, col),
        ]

    def c_copy(dy):
        at = quarter(dy)
        if dy in (0, 3):
            return remote(rbuf[ZP].at[at], rbuf[Z2].at[at], c_send.at[dy], c_recv.at[dy], down, col)
        return remote(rbuf[ZM].at[at], rbuf[Z2].at[at], c_send.at[dy], c_recv.at[dy], up, col)

    def d_copy(which, dy):
        at = quarter(dy)
        src, dst = ((ZM, PZM), (ZP, PZP), (Z2, PZ2))[which]
        return remote(rbuf[src].at[at], rbuf[dst].at[at], d_send.at[which, dy], d_recv.at[which, dy], partner, col)

    def e_copies(j):
        at = pl.ds(pl.multiple_of((y * 4 + (x + 4 - j) % 4) * CAP, CAP), CAP)
        return [
            remote(r0.at[at], rbuf[ZM].at[at], e_send.at[0, j], b_recv.at[0, 0], up, col),
            remote(r0.at[at], rbuf[ZP].at[at], e_send.at[1, j], b_recv.at[1, 0], down, col),
            remote(r0.at[at], rbuf[PART].at[at], e_send.at[2, j], b_recv.at[2, 0], partner, col),
        ]

    def fetch(step):
        return pltpu.make_async_copy(tabs.at[step], smem.at[step], smem_sem.at[step])

    def build(step, into, g):
        tiles = rbuf[step]
        for k in range(32):
            dense[into][pl.ds(pl.multiple_of(g * 16, 16), 16), k * 128 : (k + 1) * 128] = tiles[smem[step, g, 0, k]]

    def build_all(step, into, first=0, count=16):
        def body(g, carry):
            build(step, into, first + g)
            return carry

        lax.fori_loop(0, count, body, 0)

    for j in range(4):
        at = pl.ds(pl.multiple_of((y * 4 + (x + 4 - j) % 4) * CAP, CAP), CAP)
        wait_bytes(r0.at[at], e_recv.at[j])
        for copy in e_copies(j):
            copy.start()
        if j == 0:
            wait_bytes(tabs.at[OWN], ta_recv)
            for t in t_own:
                t.start()
            fetch(OWN).start()
    for dy in DYS[1:]:
        wait_bytes(r0.at[quarter(dy)], a_recv.at[dy])
        for copy in b_copies(dy):
            copy.start()
        if dy == DYS[1]:
            fetch(OWN).wait()
    build_all(OWN, 0)

    def arrived(buf, sem, dys=DYS):
        for dy in dys:
            wait_bytes(rbuf[buf].at[quarter(dy)], sem.at[dy])

    def where_from(step):
        zi = (z + OFFSET[step]) % 4
        ki = core if step in (OWN, ZM, ZP, Z2) else 1 - core
        return zi, ki

    def product(at, h, following=None):
        def columns(n, carry):
            cols = pl.ds(pl.multiple_of(n * 256, 256), 256)
            prod[:, cols] = lax.dot_general(dense[at][...], ints[cols, :], NT, preferred_element_type=jnp.float32)
            if following is not None:
                for g in range(4):
                    build(following, 1 - at, n * 4 + g)
            return carry

        lax.fori_loop(2 * h, 2 * h + 2, columns, 0)

    def q1_copies(step):
        zi, ki = where_from(step)
        d = (y + 3 - zi) % 4
        to = zi * 4 + x
        return (
            remote(q1.at[step], rq1.at[ki, d], q1_send.at[step], q1_recv.at[ki, d], row, to),
            remote(s1.at[step], rs1.at[ki, d], s1_send.at[step], s1_recv.at[ki, d], row, to),
        )

    def q2_copies(step, e):
        zi, ki = where_from(step)
        xd = 2 * ki + e
        d = (x + 3 - xd) % 4
        to = y * 4 + xd
        return (
            remote(q2.at[step, e], rq2.at[zi, d], q2_send.at[step, e], q2_recv.at[zi, d], row, to),
            remote(s2.at[step, e], rs2.at[zi, d], s2_send.at[step, e], s2_recv.at[zi, d], row, to),
        )

    def q3_copies(step, e):
        zi, ki = where_from(step)
        xd = 2 * ki + e
        d = (x + 3 - xd) % 4
        to = zi * 4 + xd
        return (
            remote(q3.at[ki, e], rq3.at[d], q3_send.at[ki, e], q3_recv.at[d], row, to),
            remote(s3.at[ki, e], rs3.at[d], s3_send.at[ki, e], s3_recv.at[d], row, to),
        )

    def q4_copies(step):
        zi, ki = where_from(step)
        d = (y + 3 - zi) % 4
        to = zi * 4 + x
        return (
            remote(q4.at[zi], rq4.at[d], q4_send.at[zi], q4_recv.at[d], row, to),
            remote(s4.at[zi], rs4.at[d], s4_send.at[zi], s4_recv.at[d], row, to),
        )

    def q5_copies(step, e):
        _, ki = where_from(step)
        xd = 2 * ki + e
        d = (x + 3 - xd) % 4
        to = y * 4 + xd
        at = 0 if step == Z2 else 1
        return (
            remote(q5.at[at, e], rq5.at[d], q5_send.at[at, e], q5_recv.at[d], row, to),
            remote(s5.at[at, e], rs5.at[d], s5_send.at[at, e], s5_recv.at[d], row, to),
        )

    def q6_copies(step):
        zi, _ = where_from(step)
        d = (y + 3 - zi) % 4
        to = zi * 4 + x
        return (
            remote(q6, rq3.at[d], q6_send, q3_recv.at[d], row, to),
            remote(s6, rs3.at[d], s6_send, s3_recv.at[d], row, to),
        )

    def move(src, dst):
        rows = src.shape[0]

        def body(r, carry):
            at = pl.ds(pl.multiple_of(r * 16, 16), 16)
            dst[at, :] = src[at, :]
            return carry

        lax.fori_loop(0, rows // 16, body, 0)

    def left_sends(step):
        zi, ki = where_from(step)
        left = prod.at[:, pl.ds(0, 512)]
        if step in (Z2, PZ2):
            for e in range(2):
                part = left.at[pl.ds(e * 128, 128), :]

                @pl.when(x != 2 * ki + e)
                def _():
                    quantize(part, q5.at[0 if step == Z2 else 1, e], s5.at[0 if step == Z2 else 1, e])
                    for copy in q5_copies(step, e):
                        copy.start()

                @pl.when(x == 2 * ki + e)
                def _():
                    move(part, acc5)

            return

        @pl.when(y != zi)
        def _():
            quantize(left, q1.at[step], s1.at[step])
            for copy in q1_copies(step):
                copy.start()

        @pl.when(y == zi)
        def _():
            move(left, acc1.at[ki])

    def right_sends(step):
        zi, ki = where_from(step)
        right = prod.at[:, pl.ds(512, 512)]
        for e in range(2):
            part = right.at[pl.ds(e * 128, 128), :]

            @pl.when(x != 2 * ki + e)
            def _():
                quantize(part, q2.at[step, e], s2.at[step, e])
                for copy in q2_copies(step, e):
                    copy.start()

            @pl.when(x == 2 * ki + e)
            def _():
                move(part, acc2.at[zi])

    def second_left(step):
        zi, ki = where_from(step)
        if step in (Z2, PZ2):

            @pl.when(x // 2 == ki)
            def _():
                for d in range(3):
                    wait_bytes(rq5.at[d], q5_recv.at[d])
                    wait_bytes(rs5.at[d], s5_recv.at[d])
                add_coded(acc5, rq5, rs5)

                @pl.when(y != zi)
                def _():
                    quantize(acc5, q6, s6)
                    for copy in q6_copies(step):
                        copy.start()

                @pl.when(y == zi)
                def _():
                    move(acc5, fin1)

            return

        @pl.when(y == zi)
        def _():
            for d in range(3):
                wait_bytes(rq1.at[ki, d], q1_recv.at[ki, d])
                wait_bytes(rs1.at[ki, d], s1_recv.at[ki, d])
            add_coded(acc1.at[ki], rq1.at[ki], rs1.at[ki])
            for e in range(2):
                part = acc1.at[ki, pl.ds(e * 128, 128), :]

                @pl.when(x != 2 * ki + e)
                def _():
                    quantize(part, q3.at[ki, e], s3.at[ki, e])
                    for copy in q3_copies(step, e):
                        copy.start()

                @pl.when(x == 2 * ki + e)
                def _():
                    move(part, fin1)

    def second_right(step):
        zi, ki = where_from(step)

        @pl.when(x // 2 == ki)
        def _():
            for d in range(3):
                wait_bytes(rq2.at[zi, d], q2_recv.at[zi, d])
                wait_bytes(rs2.at[zi, d], s2_recv.at[zi, d])
            add_coded(acc2.at[zi], rq2.at[zi], rs2.at[zi])

            @pl.when(y != zi)
            def _():
                quantize(acc2.at[zi], q4.at[zi], s4.at[zi])
                for copy in q4_copies(step):
                    copy.start()

            @pl.when(y == zi)
            def _():
                move(acc2.at[zi], fin2)

    def run(step, at, following=None):
        product(at, 0, following)
        left_sends(step)
        product(at, 1, following)
        right_sends(step)

    def second(step):
        second_left(step)
        second_right(step)

    load.wait()
    run(OWN, 0)

    wait_bytes(tabs.at[ZM], t_recv.at[ZM])
    wait_bytes(tabs.at[ZP], t_recv.at[ZP])
    t_more = [
        remote(tabs.at[ZP], tabs.at[Z2], t_send.at[3], t_recv.at[Z2], down, col),
        remote(tabs.at[ZM], tabs.at[PZM], t_send.at[4], t_recv.at[PZM], partner, col),
        remote(tabs.at[ZP], tabs.at[PZP], t_send.at[5], t_recv.at[PZP], partner, col),
    ]
    for t in t_more:
        t.start()
    wait_bytes(tabs.at[PART], t_recv.at[PART])
    for step in (PART, ZM, ZP):
        fetch(step).start()

    def pass_on(dys):
        for dy in dys:
            wait_bytes(rbuf[ZM].at[quarter(dy)], b_recv.at[0, dy])
            wait_bytes(rbuf[ZP].at[quarter(dy)], b_recv.at[1, dy])
            c_copy(dy).start()
            d_copy(0, dy).start()
            d_copy(1, dy).start()

    def pass_far(dys):
        for dy in dys:
            wait_bytes(rbuf[Z2].at[quarter(dy)], c_recv.at[dy])
            d_copy(2, dy).start()

    pass_on(DYS[:1])
    arrived(PART, b_recv.at[2])
    for step in (PART, ZM, ZP):
        fetch(step).wait()
    build_all(PART, 1)
    run(PART, 1)
    pass_on(DYS[1:])

    build_all(ZM, 0)
    run(ZM, 0, ZP)
    wait_bytes(tabs.at[PZM], t_recv.at[PZM])
    wait_bytes(tabs.at[PZP], t_recv.at[PZP])
    wait_bytes(tabs.at[Z2], t_recv.at[Z2])
    t_last = remote(tabs.at[Z2], tabs.at[PZ2], t_send.at[6], t_recv.at[PZ2], partner, col)
    t_last.start()
    for step in (PZM, PZP, Z2):
        fetch(step).start()
    arrived(PZM, d_recv.at[0])
    for step in (PZM, PZP, Z2):
        fetch(step).wait()

    run(ZP, 1, PZM)
    second(OWN)
    arrived(PZP, d_recv.at[1])
    run(PZM, 0, PZP)
    second(PART)
    pass_far(DYS)
    run(PZP, 1, Z2)
    wait_bytes(tabs.at[PZ2], t_recv.at[PZ2])
    fetch(PZ2).start()
    second(ZM)
    arrived(PZ2, d_recv.at[2])
    fetch(PZ2).wait()
    run(Z2, 0, PZ2)
    second(ZP)
    second(PZM)
    run(PZ2, 1)
    second(PZP)
    second_left(Z2)
    second_left(PZ2)
    second_right(Z2)
    second_right(PZ2)

    for d in range(3):
        wait_bytes(rq3.at[d], q3_recv.at[d])
        wait_bytes(rs3.at[d], s3_recv.at[d])
    add_coded(fin1, rq3, rs3, 0.5, out_ref.at[:, pl.ds(0, 512)])
    for d in range(3):
        wait_bytes(rq4.at[d], q4_recv.at[d])
        wait_bytes(rs4.at[d], s4_recv.at[d])
    add_coded(fin2, rq4, rs4, 0.5, out_ref.at[:, pl.ds(512, 512)])

    def table_left(j, carry):
        remote(inv_ref.at[mine], tabs.at[OWN, mine], ta_send.at[j], ta_recv, row, (col + j) % 16).wait_send()
        return carry

    lax.fori_loop(1, 16, table_left, 0)
    for t in t_own + t_more + [t_last]:
        t.wait_send()
    for dy in DYS:
        for j in range(1 if dy == 0 else 0, 4):
            tile_copy(dy, j).wait_send()
        for copy in sum((e_copies(j) for j in range(4)), []) if dy == 0 else b_copies(dy):
            copy.wait_send()
        c_copy(dy).wait_send()
        for which in range(3):
            d_copy(which, dy).wait_send()
    for step in STEPS:
        zi, ki = where_from(step)

        if step not in (Z2, PZ2):

            @pl.when(y != zi)
            def _():
                for copy in q1_copies(step):
                    copy.wait_send()

        for e in range(2):

            @pl.when(x != 2 * ki + e)
            def _():
                for copy in q2_copies(step, e):
                    copy.wait_send()
                if step in (Z2, PZ2):
                    for copy in q5_copies(step, e):
                        copy.wait_send()

            if step not in (Z2, PZ2):

                @pl.when((y == zi) & (x != 2 * ki + e))
                def _():
                    for copy in q3_copies(step, e):
                        copy.wait_send()

        @pl.when((y != zi) & (x // 2 == ki))
        def _():
            for copy in q4_copies(step):
                copy.wait_send()
            if step in (Z2, PZ2):
                for copy in q6_copies(step):
                    copy.wait_send()


def ladder(buf, inv, integrals):
    ab, cd = integrals.shape
    half = ab // 2
    i16, f32, bf16 = jnp.int16, jnp.float32, jnp.bfloat16
    dma = pltpu.SemaphoreType.DMA
    vmem = pltpu.VMEM
    scratch = [vmem((16 * CAP + 1, 16, 128), bf16) for _ in range(8)]
    scratch += [
        vmem((8, 16, 1, 128), jnp.int32), pltpu.SMEM((8, 16, 1, 128), jnp.int32),
        vmem((ab, cd), bf16), vmem((256, cd), bf16), vmem((256, cd), bf16), vmem((256, ab), f32),
        vmem((8, 256, half), i16), vmem((8, 8, 128), f32),
        vmem((8, 2, 128, half), i16), vmem((8, 2, 8, 128), f32),
        vmem((2, 2, 128, half), i16), vmem((2, 2, 8, 128), f32),
        vmem((4, 128, half), i16), vmem((4, 8, 128), f32),
        vmem((2, 3, 256, half), i16), vmem((2, 3, 8, 128), f32),
        vmem((4, 3, 128, half), i16), vmem((4, 3, 8, 128), f32),
        vmem((3, 128, half), i16), vmem((3, 8, 128), f32),
        vmem((3, 128, half), i16), vmem((3, 8, 128), f32),
        vmem((2, 2, 128, half), i16), vmem((2, 2, 8, 128), f32), vmem((3, 128, half), i16), vmem((3, 8, 128), f32),
        vmem((128, half), f32), vmem((128, half), i16), vmem((8, 128), f32),
        vmem((2, 256, half), f32), vmem((4, 128, half), f32),
        vmem((128, half), f32), vmem((128, half), f32),
        dma, dma((8,)), dma,
        dma((16,)), dma, dma((7,)), dma((8,)),
        dma((16,)), dma((4,)), dma((3, 4)), dma((3, 4)), dma((4,)), dma((4,)), dma((3, 4)), dma((3, 4)),
        dma((8,)), dma((2, 3)), dma((8, 2)), dma((4, 3)), dma((2, 2)), dma((3,)), dma((4,)), dma((3,)),
        dma((4,)), dma((3, 4)), dma((2, 2)), dma((3,)), dma((2, 2)), dma((3,)), dma, dma,
        dma((8,)), dma((2, 3)), dma((8, 2)), dma((4, 3)), dma((2, 2)), dma((3,)), dma((4,)), dma((3,)),
    ]
    any_space = pl.BlockSpec(memory_space=pl.ANY)
    return pl.pallas_call(
        ladder_kernel,
        out_shape=jax.ShapeDtypeStruct((128, ab), f32),
        in_specs=[any_space, any_space, any_space],
        out_specs=pl.BlockSpec(memory_space=pltpu.VMEM),
        scratch_shapes=scratch,
        compiler_params=pltpu.CompilerParams(collective_id=0, has_side_effects=True, vmem_limit_bytes=60 << 20),
        name="ladder",
    )(buf, inv, integrals)


def shards(lam_tiles, lam_ids, integrals):
    _, s_count, pairs, tile = lam_tiles.shape
    buf, inv = bucket(lam_ids, lam_tiles.reshape(s_count, pairs, tile), lax.axis_size("col"))
    return ladder(buf, inv, integrals)


def solution(mesh):
    return jax.shard_map(
        shards,
        mesh=mesh,
        in_specs=(P(("row", "col"), None, None, None), P(("row", "col"), None), P("row", "col")),
        out_specs=P("col", "row"),
        check_vma=False,
    )
```

```python
import functools

import jax
import jax.numpy as jnp
from jax import lax
from jax.experimental import pallas as pl
from jax.experimental.pallas import tpu as pltpu
from jax.sharding import PartitionSpec as P

CAP = 16
MESH = pl.DeviceIdType.MESH
DYS = (0, 1, 3, 2)
NT = (((1,), (1,)), ((), ()))
OWN, PART, A, B, PA, PB, Z2, PZ2 = range(8)
STEPS = (OWN, PART, A, PA, B, PB, Z2, PZ2)
Y_FIRST = {"L": (OWN, PART, A, PA, B, PB), "M": (OWN, PART, A, PA), "N": ()}
GROUP_REFS = (
    "q", "s", "rq", "rs", "acc", "q4", "s4", "rf", "rsf", "fin",
    "q_sem", "s_sem", "rq_sem", "rs_sem", "q4_sem", "s4_sem", "rf_sem", "rsf_sem",
)
Y_REFS = (
    "q1", "s1", "q3", "s3", "rq1", "rs1", "acc1",
    "q1_sem", "s1_sem", "rq1_sem", "rs1_sem", "q3_sem", "s3_sem",
)
GROUPS = {"L": (0, 256), "M": (256, 256), "N": (512, 512)}


def bucket_kernel(ids_ref, lam_ref, out_ref, inv_ref, used):
    n_col, _, _ = inv_ref.shape
    kt = 32
    first = lax.axis_index("col") * CAP

    def clear(b, carry):
        used[b] = 0
        for k in range(kt):
            inv_ref[b, 0, k] = n_col * CAP
        return carry

    lax.fori_loop(0, n_col, clear, 0)

    def body(s, carry):
        tile = ids_ref[0, s]
        b = tile // kt
        slot = used[b]
        used[b] = slot + 1
        inv_ref[b, 0, tile % kt] = first + slot
        out_ref[b * CAP + slot] = lam_ref[s]
        return carry

    lax.fori_loop(0, lam_ref.shape[0], body, 0, unroll=8)


def bucket(ids, tiles, n_col):
    return pl.pallas_call(
        bucket_kernel,
        out_shape=(
            jax.ShapeDtypeStruct((n_col * CAP,) + tiles.shape[1:], tiles.dtype),
            jax.ShapeDtypeStruct((n_col, 1, 128), jnp.int32),
        ),
        in_specs=[
            pl.BlockSpec(memory_space=pltpu.SMEM),
            pl.BlockSpec(memory_space=pltpu.VMEM),
        ],
        out_specs=(
            pl.BlockSpec(memory_space=pltpu.VMEM),
            pl.BlockSpec(memory_space=pltpu.SMEM),
        ),
        scratch_shapes=[pltpu.SMEM((n_col,), jnp.int32)],
        name="bucket",
    )(ids, tiles)


def wide(scale, width):
    return jnp.concatenate([jnp.concatenate([scale, scale], axis=0)] * (width // 128), axis=1)


def quantize(src, dst, scale_dst):
    rows, width = src.shape

    def largest(r, m):
        a = jnp.abs(src[pl.ds(r * 16, 16), :])
        for j in range(width // 128):
            part = a[:, j * 128 : (j + 1) * 128]
            m = jnp.maximum(m, jnp.maximum(part[:8], part[8:]))
        return m

    m = lax.fori_loop(0, rows // 16, largest, jnp.zeros((8, 128), jnp.float32), unroll=2)
    scale_dst[...] = m * (1.0 / 32767.0)
    inverse = wide(jnp.where(m > 0.0, 32767.0 / m, 0.0), width)

    def code(r, carry):
        at = pl.ds(pl.multiple_of(r * 16, 16), 16)
        dst[at, :] = jnp.round(src[at, :] * inverse).astype(jnp.int32).astype(jnp.int16)
        return carry

    lax.fori_loop(0, rows // 16, code, 0, unroll=2)


def add_coded(acc, coded, scales, factor=None, out=None):
    rows, width = acc.shape
    w = [wide(scales[j], width) for j in range(3)]

    def body(r, carry):
        at = pl.ds(pl.multiple_of(r * 16, 16), 16)
        total = acc[at, :]
        for j in range(3):
            total = total + coded[j, at, :].astype(jnp.int32).astype(jnp.float32) * w[j]
        if out is None:
            acc[at, :] = total
        else:
            out[at, :] = factor * total
        return carry

    lax.fori_loop(0, rows // 16, body, 0, unroll=2)


def ladder_kernel(
    buf_ref, inv_ref, int_ref, out_ref,
    r0, r1, r2, r3, r4, r5, r6, r7, tabs, smem, ints, dense0, dense1, prod,
    int_sem, smem_sem, e_recv, e_send,
    ta_send, ta_recv, t_send, t_recv,
    a_send, a_recv, b_send, b_recv, c_send, c_recv, d_send, d_recv,
    *by_group
):
    refs = {g: dict(zip(GROUP_REFS, by_group[i * len(GROUP_REFS) :])) for i, g in enumerate(GROUPS)}
    for i, g in enumerate("LM"):
        refs[g].update(zip(Y_REFS, by_group[len(GROUPS) * len(GROUP_REFS) + i * len(Y_REFS) :]))
    dense = (dense0, dense1)
    rbuf = (r0, r1, r2, r3, r4, r5, r6, r7)
    row, col = lax.axis_index("row"), lax.axis_index("col")
    z, core = row // 2, row % 2
    y, x = col // 4, col % 4
    up = ((z + 1) % 4) * 2 + core
    down = ((z + 3) % 4) * 2 + core
    partner = z * 2 + (1 - core)
    first_row = jnp.where(core == 0, up, down)
    second_row = jnp.where(core == 0, down, up)

    barrier = pltpu.get_barrier_semaphore()

    def greet(j, carry):
        pl.semaphore_signal(barrier, inc=1, device_id={"row": row, "col": (col + j) % 16}, device_id_type=MESH)
        return carry

    lax.fori_loop(1, 16, greet, 0)
    for other in (up, down, partner):
        pl.semaphore_signal(barrier, inc=1, device_id={"row": other, "col": col}, device_id_type=MESH)
    pl.semaphore_wait(barrier, 18)

    def remote(src, dst, send, recv, to_row, to_col):
        return pltpu.make_async_remote_copy(
            src_ref=src, dst_ref=dst, send_sem=send, recv_sem=recv,
            device_id={"row": to_row, "col": to_col}, device_id_type=MESH,
        )

    def wait_bytes(ref, sem):
        pltpu.make_async_copy(ref, ref, sem).wait()

    load = pltpu.make_async_copy(int_ref, ints, int_sem)

    mine = pl.ds(col, 1)
    own_table = pltpu.make_async_copy(inv_ref.at[mine], tabs.at[OWN, mine], ta_recv)
    own_table.start()

    def send_table(j, carry):
        to = (col + j) % 16
        remote(inv_ref.at[pl.ds(to, 1)], tabs.at[OWN, mine], ta_send.at[j], ta_recv, row, to).start()
        return carry

    lax.fori_loop(1, 16, send_table, 0)

    here = pl.ds(pl.multiple_of(col * CAP, CAP), CAP)
    pltpu.make_async_copy(buf_ref.at[here], r0.at[here], e_recv.at[0]).start()

    def tile_copy(dy, j):
        to = ((y + 4 - dy) % 4) * 4 + (x + j) % 4
        there = pl.ds(pl.multiple_of(to * CAP, CAP), CAP)
        arrival = e_recv.at[j] if dy == 0 else a_recv.at[dy]
        return remote(buf_ref.at[there], r0.at[here], a_send.at[dy * 4 + j], arrival, row, to)

    for dy in DYS:
        for j in range(1 if dy == 0 else 0, 4):
            tile_copy(dy, j).start()
    load.start()

    zero = jnp.zeros((16, 128), jnp.bfloat16)
    for r in rbuf:
        r[16 * CAP] = zero

    t_own = [
        remote(tabs.at[OWN], tabs.at[A], t_send.at[0], t_recv.at[A], first_row, col),
        remote(tabs.at[OWN], tabs.at[B], t_send.at[1], t_recv.at[B], second_row, col),
        remote(tabs.at[OWN], tabs.at[PART], t_send.at[2], t_recv.at[PART], partner, col),
    ]

    def quarter(dy):
        return pl.ds(pl.multiple_of(((y + dy) % 4) * 4 * CAP, 4 * CAP), 4 * CAP)

    def b_copies(dy, which):
        at = quarter(dy)
        to, buf = ((first_row, A), (second_row, B), (partner, PART))[which]
        return remote(r0.at[at], rbuf[buf].at[at], b_send.at[which, dy], b_recv.at[which, dy], to, col)

    def c_copy(dy):
        at = quarter(dy)
        return remote(rbuf[A].at[at], rbuf[Z2].at[at], c_send.at[dy], c_recv.at[dy], first_row, col)

    def d_copy(which, dy):
        at = quarter(dy)
        src, dst = ((A, PA), (B, PB), (Z2, PZ2))[which]
        return remote(rbuf[src].at[at], rbuf[dst].at[at], d_send.at[which, dy], d_recv.at[which, dy], partner, col)

    def block(j):
        return pl.ds(pl.multiple_of((y * 4 + (x + 4 - j) % 4) * CAP, CAP), CAP)

    def e_copy(j, which):
        at = block(j)
        to, buf = ((first_row, A), (second_row, B), (partner, PART))[which]
        return remote(r0.at[at], rbuf[buf].at[at], e_send.at[which, j], b_recv.at[which, 0], to, col)

    def fetch(step):
        return pltpu.make_async_copy(tabs.at[step], smem.at[step], smem_sem.at[step])

    def build(step, into, g):
        tiles = rbuf[step]
        for k in range(32):
            dense[into][pl.ds(pl.multiple_of(g * 16, 16), 16), k * 128 : (k + 1) * 128] = tiles[smem[step, g, 0, k]]

    def build_all(step, into, first=0, count=16):
        def body(g, carry):
            build(step, into, first + g)
            return carry

        lax.fori_loop(0, count, body, 0)

    for j in range(4):
        wait_bytes(r0.at[block(j)], e_recv.at[j])
        e_copy(j, 0).start()
        e_copy(j, 2).start()
        if j == 0:
            wait_bytes(tabs.at[OWN], ta_recv)
            for t in t_own:
                t.start()
            fetch(OWN).start()
    for dy in DYS[1:]:
        wait_bytes(r0.at[quarter(dy)], a_recv.at[dy])
        b_copies(dy, 0).start()
        b_copies(dy, 2).start()
        if dy == DYS[1]:
            fetch(OWN).wait()

    def to_second():
        for j in range(4):
            e_copy(j, 1).start()
        for dy in DYS[1:]:
            b_copies(dy, 1).start()

    pl.when(core == 0)(to_second)
    build_all(OWN, 0)

    def arrived(buf, sem, dys=DYS):
        for dy in dys:
            wait_bytes(rbuf[buf].at[quarter(dy)], sem.at[dy])

    def where_from(step):
        ahead, behind = jnp.where(core == 0, 3, 1), jnp.where(core == 0, 1, 3)
        offset = {OWN: 0, PART: 0, A: ahead, PB: ahead, B: behind, PA: behind, Z2: 2, PZ2: 2}[step]
        return (z + offset) % 4, core if step in (OWN, A, B, Z2) else 1 - core

    def product(at, h):
        cols = pl.ds(512 * h, 512)
        prod[:, cols] = lax.dot_general(dense[at][...], ints[cols, :], NT, preferred_element_type=jnp.float32)

    def q1_copies(step, group):
        zi, ki = where_from(step)
        d = (y + 3 - zi) % 4
        r, to = refs[group], zi * 4 + x
        return (
            remote(r["q1"].at[step], r["rq1"].at[ki, d], r["q1_sem"].at[step], r["rq1_sem"].at[ki, d], row, to),
            remote(r["s1"].at[step], r["rs1"].at[ki, d], r["s1_sem"].at[step], r["rs1_sem"].at[ki, d], row, to),
        )

    def place_of(step, group):
        return (int(step == PZ2), 0) if group == "L" else (step, where_from(step)[0])

    def x_copies(step, group, e):
        _, ki = where_from(step)
        d = (x + 3 - (2 * ki + e)) % 4
        r, (at, slot), to = refs[group], place_of(step, group), y * 4 + 2 * ki + e
        return (
            remote(r["q"].at[at, e], r["rq"].at[slot, d], r["q_sem"].at[at, e], r["rq_sem"].at[slot, d], row, to),
            remote(r["s"].at[at, e], r["rs"].at[slot, d], r["s_sem"].at[at, e], r["rs_sem"].at[slot, d], row, to),
        )

    def q3_copies(step, group, e):
        zi, ki = where_from(step)
        xd = 2 * ki + e
        d = (x + 3 - xd) % 4
        r, to = refs[group], zi * 4 + xd
        return (
            remote(r["q3"].at[ki, e], r["rf"].at[d], r["q3_sem"].at[ki, e], r["rf_sem"].at[d], row, to),
            remote(r["s3"].at[ki, e], r["rsf"].at[d], r["s3_sem"].at[ki, e], r["rsf_sem"].at[d], row, to),
        )

    def y_copies(step, group):
        zi, _ = where_from(step)
        d = (y + 3 - zi) % 4
        r, (_, slot), to = refs[group], place_of(step, group), zi * 4 + x
        return (
            remote(r["q4"].at[slot], r["rf"].at[d], r["q4_sem"].at[slot], r["rf_sem"].at[d], row, to),
            remote(r["s4"].at[slot], r["rsf"].at[d], r["s4_sem"].at[slot], r["rsf_sem"].at[d], row, to),
        )

    def move(src, dst):
        rows = src.shape[0]

        def body(r, carry):
            at = pl.ds(pl.multiple_of(r * 16, 16), 16)
            dst[at, :] = src[at, :]
            return carry

        lax.fori_loop(0, rows // 16, body, 0)

    def x_first(step, group):
        _, ki = where_from(step)
        start, width = GROUPS[group]
        r, (at, slot) = refs[group], place_of(step, group)
        for e in range(2):
            part = prod.at[pl.ds(e * 128, 128), pl.ds(start, width)]

            @pl.when(x != 2 * ki + e)
            def _():
                quantize(part, r["q"].at[at, e], r["s"].at[at, e])
                for copy in x_copies(step, group, e):
                    copy.start()

            @pl.when(x == 2 * ki + e)
            def _():
                move(part, r["acc"].at[slot])

    def y_second(step, group):
        zi, ki = where_from(step)
        r, (_, slot) = refs[group], place_of(step, group)

        @pl.when(x // 2 == ki)
        def _():
            for d in range(3):
                wait_bytes(r["rq"].at[slot, d], r["rq_sem"].at[slot, d])
                wait_bytes(r["rs"].at[slot, d], r["rs_sem"].at[slot, d])

            @pl.when(y != zi)
            def _():
                add_coded(r["acc"].at[slot], r["rq"].at[slot], r["rs"].at[slot])
                quantize(r["acc"].at[slot], r["q4"].at[slot], r["s4"].at[slot])
                for copy in y_copies(step, group):
                    copy.start()

            @pl.when(y == zi)
            def _():
                add_coded(r["acc"].at[slot], r["rq"].at[slot], r["rs"].at[slot], 1.0, r["fin"])

    def y_first(step, group):
        zi, ki = where_from(step)
        r, part = refs[group], prod.at[:, pl.ds(*GROUPS[group])]

        @pl.when(y != zi)
        def _():
            quantize(part, r["q1"].at[step], r["s1"].at[step])
            for copy in q1_copies(step, group):
                copy.start()

        @pl.when(y == zi)
        def _():
            move(part, r["acc1"].at[ki])

    def x_second(step, group):
        zi, ki = where_from(step)
        r = refs[group]

        @pl.when(y == zi)
        def _():
            for d in range(3):
                wait_bytes(r["rq1"].at[ki, d], r["rq1_sem"].at[ki, d])
                wait_bytes(r["rs1"].at[ki, d], r["rs1_sem"].at[ki, d])
            add_coded(r["acc1"].at[ki], r["rq1"].at[ki], r["rs1"].at[ki])
            for e in range(2):
                part = r["acc1"].at[ki, pl.ds(e * 128, 128), :]

                @pl.when(x != 2 * ki + e)
                def _():
                    quantize(part, r["q3"].at[ki, e], r["s3"].at[ki, e])
                    for copy in q3_copies(step, group, e):
                        copy.start()

                @pl.when(x == 2 * ki + e)
                def _():
                    move(part, r["fin"])

    def send(step, group):
        (y_first if step in Y_FIRST[group] else x_first)(step, group)

    def pass_sums(step, group):
        (x_second if step in Y_FIRST[group] else y_second)(step, group)

    def run(step, at):
        product(at, 1)
        send(step, "N")
        product(at, 0)
        send(step, "L")
        send(step, "M")

    load.wait()
    run(OWN, 0)

    @pl.when(core == 1)
    def _():
        to_second()

    for step in (A, B, PART):
        wait_bytes(tabs.at[step], t_recv.at[step])
        fetch(step).start()
    t_more = [
        remote(tabs.at[A], tabs.at[Z2], t_send.at[3], t_recv.at[Z2], first_row, col),
        remote(tabs.at[A], tabs.at[PA], t_send.at[4], t_recv.at[PA], partner, col),
        remote(tabs.at[B], tabs.at[PB], t_send.at[5], t_recv.at[PB], partner, col),
    ]
    for t in t_more:
        t.start()

    def pass_on(which, dys=DYS):
        for dy in dys:
            wait_bytes(rbuf[(A, B)[which]].at[quarter(dy)], b_recv.at[which, dy])
            d_copy(which, dy).start()
            if which == 1:
                c_copy(dy).start()

    def pass_far(dys):
        for dy in dys:
            wait_bytes(rbuf[Z2].at[quarter(dy)], c_recv.at[dy])
            d_copy(2, dy).start()

    pass_on(0, DYS[:2])
    arrived(PART, b_recv.at[2])
    for step in (A, B, PART):
        fetch(step).wait()
    build_all(PART, 1)
    run(PART, 1)
    pass_on(0, DYS[2:])
    for step in (PA, PB, Z2):
        wait_bytes(tabs.at[step], t_recv.at[step])
        fetch(step).start()
    t_last = remote(tabs.at[Z2], tabs.at[PZ2], t_send.at[6], t_recv.at[PZ2], partner, col)
    t_last.start()
    build_all(A, 0)
    run(A, 0)
    pass_sums(OWN, "N")
    for step in (PA, PB, Z2):
        fetch(step).wait()
    pass_on(1, DYS[:2])
    arrived(PA, d_recv.at[0])
    build_all(PA, 1)
    run(PA, 1)
    pass_sums(PART, "N")
    pass_on(1, DYS[2:])
    build_all(B, 0)
    run(B, 0)
    pass_sums(OWN, "L")
    pass_sums(OWN, "M")
    pass_sums(A, "N")
    arrived(PB, d_recv.at[1])
    build_all(PB, 1)
    run(PB, 1)
    pass_sums(PART, "L")
    pass_sums(PART, "M")
    pass_sums(PA, "N")
    pass_far(DYS)
    wait_bytes(tabs.at[PZ2], t_recv.at[PZ2])
    fetch(PZ2).start()
    build_all(Z2, 0)
    run(Z2, 0)
    pass_sums(B, "N")
    pass_sums(B, "M")
    pass_sums(A, "L")
    arrived(PZ2, d_recv.at[2])
    fetch(PZ2).wait()
    build_all(PZ2, 1)
    product(1, 1)
    send(PZ2, "N")
    pass_sums(A, "M")
    product(1, 0)
    send(PZ2, "L")
    send(PZ2, "M")
    pass_sums(PA, "L")
    pass_sums(PA, "M")
    pass_sums(PB, "N")
    pass_sums(PB, "M")
    pass_sums(B, "L")
    pass_sums(Z2, "N")
    pass_sums(PB, "L")
    pass_sums(Z2, "L")
    pass_sums(Z2, "M")
    pass_sums(PZ2, "N")
    pass_sums(PZ2, "L")
    pass_sums(PZ2, "M")

    for group in ("N", "L", "M"):
        r, (start, width) = refs[group], GROUPS[group]
        for d in range(3):
            wait_bytes(r["rf"].at[d], r["rf_sem"].at[d])
            wait_bytes(r["rsf"].at[d], r["rsf_sem"].at[d])
        add_coded(r["fin"], r["rf"], r["rsf"], 0.5, out_ref.at[:, pl.ds(start, width)])

    def table_left(j, carry):
        remote(inv_ref.at[mine], tabs.at[OWN, mine], ta_send.at[j], ta_recv, row, (col + j) % 16).wait_send()
        return carry

    lax.fori_loop(1, 16, table_left, 0)
    for t in t_own + t_more + [t_last]:
        t.wait_send()
    for dy in DYS:
        for j in range(1 if dy == 0 else 0, 4):
            tile_copy(dy, j).wait_send()
        for which in range(3):
            for copy in [e_copy(j, which) for j in range(4)] if dy == 0 else [b_copies(dy, which)]:
                copy.wait_send()
        c_copy(dy).wait_send()
        for which in range(3):
            d_copy(which, dy).wait_send()
    for step in STEPS:
        zi, ki = where_from(step)
        y_groups = [g for g in GROUPS if step in Y_FIRST[g]]
        x_groups = [g for g in GROUPS if step not in Y_FIRST[g]]

        @pl.when(y != zi)
        def _():
            for group in y_groups:
                for copy in q1_copies(step, group):
                    copy.wait_send()

        for e in range(2):

            @pl.when((y == zi) & (x != 2 * ki + e))
            def _():
                for group in y_groups:
                    for copy in q3_copies(step, group, e):
                        copy.wait_send()

            @pl.when(x != 2 * ki + e)
            def _():
                for group in x_groups:
                    for copy in x_copies(step, group, e):
                        copy.wait_send()

        @pl.when((y != zi) & (x // 2 == ki))
        def _():
            for group in x_groups:
                for copy in y_copies(step, group):
                    copy.wait_send()


def ladder(buf, inv, integrals):
    ab, cd = integrals.shape
    i16, f32, bf16 = jnp.int16, jnp.float32, jnp.bfloat16
    dma = pltpu.SemaphoreType.DMA
    vmem = pltpu.VMEM
    scratch = [vmem((16 * CAP + 1, 16, 128), bf16) for _ in range(8)]
    scratch += [
        vmem((8, 16, 1, 128), jnp.int32), pltpu.SMEM((8, 16, 1, 128), jnp.int32),
        vmem((ab, cd), bf16), vmem((256, cd), bf16), vmem((256, cd), bf16), vmem((256, ab), f32),
        dma, dma((8,)), dma((4,)), dma((3, 4)),
        dma((16,)), dma, dma((7,)), dma((8,)),
        dma((16,)), dma((4,)), dma((3, 4)), dma((3, 4)), dma((4,)), dma((4,)), dma((3, 4)), dma((3, 4)),
    ]
    for group, (_, width) in GROUPS.items():
        steps, slots = (2, 1) if group == "L" else (8, 4)
        scratch += [
            vmem((steps, 2, 128, width), i16), vmem((steps, 2, 8, 128), f32),
            vmem((slots, 3, 128, width), i16), vmem((slots, 3, 8, 128), f32), vmem((slots, 128, width), f32),
            vmem((slots, 128, width), i16), vmem((slots, 8, 128), f32),
            vmem((3, 128, width), i16), vmem((3, 8, 128), f32), vmem((128, width), f32),
            dma((steps, 2)), dma((steps, 2)), dma((slots, 3)), dma((slots, 3)), dma((slots,)), dma((slots,)), dma((3,)), dma((3,)),
        ]
    for _ in "LM":
        scratch += [
            vmem((8, 256, 256), i16), vmem((8, 8, 128), f32), vmem((2, 2, 128, 256), i16), vmem((2, 2, 8, 128), f32),
            vmem((2, 3, 256, 256), i16), vmem((2, 3, 8, 128), f32), vmem((2, 256, 256), f32),
            dma((8,)), dma((8,)), dma((2, 3)), dma((2, 3)), dma((2, 2)), dma((2, 2)),
        ]
    any_space = pl.BlockSpec(memory_space=pl.ANY)
    return pl.pallas_call(
        ladder_kernel,
        out_shape=jax.ShapeDtypeStruct((128, ab), f32),
        in_specs=[any_space, any_space, any_space],
        out_specs=pl.BlockSpec(memory_space=pltpu.VMEM),
        scratch_shapes=scratch,
        compiler_params=pltpu.CompilerParams(collective_id=0, has_side_effects=True, vmem_limit_bytes=60 << 20),
        name="ladder",
    )(buf, inv, integrals)


def shards(lam_tiles, lam_ids, integrals):
    _, s_count, pairs, tile = lam_tiles.shape
    buf, inv = bucket(lam_ids, lam_tiles.reshape(s_count, pairs, tile), lax.axis_size("col"))
    return ladder(buf, inv, integrals)


def solution(mesh):
    return jax.shard_map(
        shards,
        mesh=mesh,
        in_specs=(P(("row", "col"), None, None, None), P(("row", "col"), None), P("row", "col")),
        out_specs=P("col", "row"),
        check_vma=False,
    )
```

```python
import functools

import jax
import jax.numpy as jnp
from jax import lax
from jax.experimental import pallas as pl
from jax.experimental.pallas import tpu as pltpu
from jax.sharding import PartitionSpec as P

CAP = 16
MESH = pl.DeviceIdType.MESH
DYS = (0, 1, 3, 2)
NT = (((1,), (1,)), ((), ()))
OWN, PART, A, B, PA, PB, Z2, PZ2 = range(8)
STEPS = (OWN, PART, A, PA, B, PB, Z2, PZ2)
Y_FIRST = {"L": (OWN, PART, A, PA, B, PB), "M": (OWN, PART, A, PA), "N": ()}
GROUP_REFS = (
    "q", "s", "rq", "rs", "acc", "q4", "s4", "rf", "rsf", "fin",
    "q_sem", "s_sem", "rq_sem", "rs_sem", "q4_sem", "s4_sem", "rf_sem", "rsf_sem",
)
Y_REFS = (
    "q1", "s1", "q3", "s3", "rq1", "rs1", "acc1",
    "q1_sem", "s1_sem", "rq1_sem", "rs1_sem", "q3_sem", "s3_sem",
)
GROUPS = {"L": (0, 256), "M": (256, 256), "N": (512, 512)}


def bucket_kernel(ids_ref, lam_ref, out_ref, inv_ref, used, place, tiles, sem):
    n_col, _, _ = inv_ref.shape
    kt = 32
    own = lax.axis_index("col") * CAP
    load = pltpu.make_async_copy(lam_ref, tiles, sem)
    load.start()

    def clear(b, carry):
        used[b] = 0
        for k in range(kt):
            inv_ref[b, 0, k] = n_col * CAP
        return carry

    lax.fori_loop(0, n_col, clear, 0)

    def find(s, carry):
        tile = ids_ref[0, s]
        b = tile // kt
        slot = used[b]
        used[b] = slot + 1
        inv_ref[b, 0, tile % kt] = own + slot
        place[s] = b * CAP + slot
        return carry

    lax.fori_loop(0, tiles.shape[0], find, 0, unroll=8)
    load.wait()

    def put(s, carry):
        out_ref[place[s]] = tiles[s]
        return carry

    lax.fori_loop(0, tiles.shape[0], put, 0, unroll=8)


def bucket(ids, tiles, n_col):
    return pl.pallas_call(
        bucket_kernel,
        out_shape=(
            jax.ShapeDtypeStruct((n_col * CAP,) + tiles.shape[1:], tiles.dtype),
            jax.ShapeDtypeStruct((n_col, 1, 128), jnp.int32),
        ),
        in_specs=[
            pl.BlockSpec(memory_space=pltpu.SMEM),
            pl.BlockSpec(memory_space=pl.ANY),
        ],
        out_specs=(
            pl.BlockSpec(memory_space=pltpu.VMEM),
            pl.BlockSpec(memory_space=pltpu.SMEM),
        ),
        scratch_shapes=[
            pltpu.SMEM((n_col,), jnp.int32),
            pltpu.SMEM((tiles.shape[0],), jnp.int32),
            pltpu.VMEM(tiles.shape, tiles.dtype),
            pltpu.SemaphoreType.DMA,
        ],
        name="bucket",
    )(ids, tiles)


def wide(scale, width):
    return jnp.concatenate([jnp.concatenate([scale, scale], axis=0)] * (width // 128), axis=1)


def quantize(src, dst, scale_dst):
    rows, width = src.shape

    def largest(r, m):
        a = jnp.abs(src[pl.ds(r * 16, 16), :])
        for j in range(width // 128):
            part = a[:, j * 128 : (j + 1) * 128]
            m = jnp.maximum(m, jnp.maximum(part[:8], part[8:]))
        return m

    m = lax.fori_loop(0, rows // 16, largest, jnp.zeros((8, 128), jnp.float32), unroll=2)
    scale_dst[...] = m * (1.0 / 32767.0)
    inverse = wide(jnp.where(m > 0.0, 32767.0 / m, 0.0), width)

    def code(r, carry):
        at = pl.ds(pl.multiple_of(r * 16, 16), 16)
        dst[at, :] = jnp.round(src[at, :] * inverse).astype(jnp.int32).astype(jnp.int16)
        return carry

    lax.fori_loop(0, rows // 16, code, 0, unroll=2)


def add_coded(acc, coded, scales, factor=None, out=None):
    rows, width = acc.shape
    w = [wide(scales[j], width) for j in range(3)]

    def body(r, carry):
        at = pl.ds(pl.multiple_of(r * 16, 16), 16)
        total = acc[at, :]
        for j in range(3):
            total = total + coded[j, at, :].astype(jnp.int32).astype(jnp.float32) * w[j]
        if out is None:
            acc[at, :] = total
        else:
            out[at, :] = factor * total
        return carry

    lax.fori_loop(0, rows // 16, body, 0, unroll=2)


def ladder_kernel(
    buf_ref, inv_ref, int_ref, out_ref,
    r0, r1, r2, r3, r4, r5, r6, r7, tabs, smem, ints, dense0, dense1, prod,
    int_sem, smem_sem, e_recv, e_send,
    ta_send, ta_recv, t_send, t_recv,
    a_send, a_recv, b_send, b_recv, c_send, c_recv, d_send, d_recv,
    *by_group
):
    refs = {g: dict(zip(GROUP_REFS, by_group[i * len(GROUP_REFS) :])) for i, g in enumerate(GROUPS)}
    for i, g in enumerate("LM"):
        refs[g].update(zip(Y_REFS, by_group[len(GROUPS) * len(GROUP_REFS) + i * len(Y_REFS) :]))
    dense = (dense0, dense1)
    rbuf = (r0, r1, r2, r3, r4, r5, r6, r7)
    row, col = lax.axis_index("row"), lax.axis_index("col")
    z, core = row // 2, row % 2
    y, x = col // 4, col % 4
    up = ((z + 1) % 4) * 2 + core
    down = ((z + 3) % 4) * 2 + core
    partner = z * 2 + (1 - core)
    first_row = jnp.where(core == 0, up, down)
    second_row = jnp.where(core == 0, down, up)

    barrier = pltpu.get_barrier_semaphore()

    def greet(j, carry):
        pl.semaphore_signal(barrier, inc=1, device_id={"row": row, "col": (col + j) % 16}, device_id_type=MESH)
        return carry

    lax.fori_loop(1, 16, greet, 0)
    for other in (up, down, partner):
        pl.semaphore_signal(barrier, inc=1, device_id={"row": other, "col": col}, device_id_type=MESH)
    pl.semaphore_wait(barrier, 18)

    def remote(src, dst, send, recv, to_row, to_col):
        return pltpu.make_async_remote_copy(
            src_ref=src, dst_ref=dst, send_sem=send, recv_sem=recv,
            device_id={"row": to_row, "col": to_col}, device_id_type=MESH,
        )

    def wait_bytes(ref, sem):
        pltpu.make_async_copy(ref, ref, sem).wait()

    load = pltpu.make_async_copy(int_ref, ints, int_sem)

    mine = pl.ds(col, 1)
    own_table = pltpu.make_async_copy(inv_ref.at[mine], tabs.at[OWN, mine], ta_recv)
    own_table.start()

    def send_table(j, carry):
        to = (col + j) % 16
        remote(inv_ref.at[pl.ds(to, 1)], tabs.at[OWN, mine], ta_send.at[j], ta_recv, row, to).start()
        return carry

    lax.fori_loop(1, 16, send_table, 0)

    here = pl.ds(pl.multiple_of(col * CAP, CAP), CAP)
    pltpu.make_async_copy(buf_ref.at[here], r0.at[here], e_recv.at[0]).start()

    def tile_copy(dy, j):
        to = ((y + 4 - dy) % 4) * 4 + (x + j) % 4
        there = pl.ds(pl.multiple_of(to * CAP, CAP), CAP)
        arrival = e_recv.at[j] if dy == 0 else a_recv.at[dy]
        return remote(buf_ref.at[there], r0.at[here], a_send.at[dy * 4 + j], arrival, row, to)

    for dy in DYS:
        for j in range(1 if dy == 0 else 0, 4):
            tile_copy(dy, j).start()
    load.start()

    zero = jnp.zeros((16, 128), jnp.bfloat16)
    for r in rbuf:
        r[16 * CAP] = zero

    t_own = [
        remote(tabs.at[OWN], tabs.at[A], t_send.at[0], t_recv.at[A], first_row, col),
        remote(tabs.at[OWN], tabs.at[B], t_send.at[1], t_recv.at[B], second_row, col),
        remote(tabs.at[OWN], tabs.at[PART], t_send.at[2], t_recv.at[PART], partner, col),
    ]

    def quarter(dy):
        return pl.ds(pl.multiple_of(((y + dy) % 4) * 4 * CAP, 4 * CAP), 4 * CAP)

    def b_copies(dy, which):
        at = quarter(dy)
        to, buf = ((first_row, A), (second_row, B), (partner, PART))[which]
        return remote(r0.at[at], rbuf[buf].at[at], b_send.at[which, dy], b_recv.at[which, dy], to, col)

    def c_copy(dy):
        at = quarter(dy)
        return remote(rbuf[A].at[at], rbuf[Z2].at[at], c_send.at[dy], c_recv.at[dy], first_row, col)

    def d_copy(which, dy):
        at = quarter(dy)
        src, dst = ((A, PA), (B, PB), (Z2, PZ2))[which]
        return remote(rbuf[src].at[at], rbuf[dst].at[at], d_send.at[which, dy], d_recv.at[which, dy], partner, col)

    def block(j):
        return pl.ds(pl.multiple_of((y * 4 + (x + 4 - j) % 4) * CAP, CAP), CAP)

    def e_copy(j, which):
        at = block(j)
        to, buf = ((first_row, A), (second_row, B), (partner, PART))[which]
        return remote(r0.at[at], rbuf[buf].at[at], e_send.at[which, j], b_recv.at[which, 0], to, col)

    def fetch(step):
        return pltpu.make_async_copy(tabs.at[step], smem.at[step], smem_sem.at[step])

    def build(step, into, g):
        tiles = rbuf[step]
        for k in range(32):
            dense[into][pl.ds(pl.multiple_of(g * 16, 16), 16), k * 128 : (k + 1) * 128] = tiles[smem[step, g, 0, k]]

    def build_all(step, into, first=0, count=16):
        def body(g, carry):
            build(step, into, first + g)
            return carry

        lax.fori_loop(0, count, body, 0)

    for j in range(4):
        wait_bytes(r0.at[block(j)], e_recv.at[j])
        e_copy(j, 0).start()
        e_copy(j, 2).start()
        if j == 0:
            wait_bytes(tabs.at[OWN], ta_recv)
            for t in t_own:
                t.start()
            fetch(OWN).start()
    for dy in DYS[1:]:
        wait_bytes(r0.at[quarter(dy)], a_recv.at[dy])
        b_copies(dy, 0).start()
        b_copies(dy, 2).start()
        if dy == DYS[1]:
            fetch(OWN).wait()

    def to_second():
        for j in range(4):
            e_copy(j, 1).start()
        for dy in DYS[1:]:
            b_copies(dy, 1).start()

    pl.when(core == 0)(to_second)
    build_all(OWN, 0)

    def arrived(buf, sem, dys=DYS):
        for dy in dys:
            wait_bytes(rbuf[buf].at[quarter(dy)], sem.at[dy])

    def where_from(step):
        ahead, behind = jnp.where(core == 0, 3, 1), jnp.where(core == 0, 1, 3)
        offset = {OWN: 0, PART: 0, A: ahead, PB: ahead, B: behind, PA: behind, Z2: 2, PZ2: 2}[step]
        return (z + offset) % 4, core if step in (OWN, A, B, Z2) else 1 - core

    def product(at, h):
        cols = pl.ds(512 * h, 512)
        prod[:, cols] = lax.dot_general(dense[at][...], ints[cols, :], NT, preferred_element_type=jnp.float32)

    def q1_copies(step, group):
        zi, ki = where_from(step)
        d = (y + 3 - zi) % 4
        r, to = refs[group], zi * 4 + x
        return (
            remote(r["q1"].at[step], r["rq1"].at[ki, d], r["q1_sem"].at[step], r["rq1_sem"].at[ki, d], row, to),
            remote(r["s1"].at[step], r["rs1"].at[ki, d], r["s1_sem"].at[step], r["rs1_sem"].at[ki, d], row, to),
        )

    def place_of(step, group):
        return (int(step == PZ2), 0) if group == "L" else (step, where_from(step)[0])

    def x_copies(step, group, e):
        _, ki = where_from(step)
        d = (x + 3 - (2 * ki + e)) % 4
        r, (at, slot), to = refs[group], place_of(step, group), y * 4 + 2 * ki + e
        return (
            remote(r["q"].at[at, e], r["rq"].at[slot, d], r["q_sem"].at[at, e], r["rq_sem"].at[slot, d], row, to),
            remote(r["s"].at[at, e], r["rs"].at[slot, d], r["s_sem"].at[at, e], r["rs_sem"].at[slot, d], row, to),
        )

    def q3_copies(step, group, e):
        zi, ki = where_from(step)
        xd = 2 * ki + e
        d = (x + 3 - xd) % 4
        r, to = refs[group], zi * 4 + xd
        return (
            remote(r["q3"].at[ki, e], r["rf"].at[d], r["q3_sem"].at[ki, e], r["rf_sem"].at[d], row, to),
            remote(r["s3"].at[ki, e], r["rsf"].at[d], r["s3_sem"].at[ki, e], r["rsf_sem"].at[d], row, to),
        )

    def y_copies(step, group):
        zi, _ = where_from(step)
        d = (y + 3 - zi) % 4
        r, (_, slot), to = refs[group], place_of(step, group), zi * 4 + x
        return (
            remote(r["q4"].at[slot], r["rf"].at[d], r["q4_sem"].at[slot], r["rf_sem"].at[d], row, to),
            remote(r["s4"].at[slot], r["rsf"].at[d], r["s4_sem"].at[slot], r["rsf_sem"].at[d], row, to),
        )

    def move(src, dst):
        rows = src.shape[0]

        def body(r, carry):
            at = pl.ds(pl.multiple_of(r * 16, 16), 16)
            dst[at, :] = src[at, :]
            return carry

        lax.fori_loop(0, rows // 16, body, 0)

    def x_first(step, group):
        _, ki = where_from(step)
        start, width = GROUPS[group]
        r, (at, slot) = refs[group], place_of(step, group)
        for e in range(2):
            part = prod.at[pl.ds(e * 128, 128), pl.ds(start, width)]

            @pl.when(x != 2 * ki + e)
            def _():
                quantize(part, r["q"].at[at, e], r["s"].at[at, e])
                for copy in x_copies(step, group, e):
                    copy.start()

            @pl.when(x == 2 * ki + e)
            def _():
                move(part, r["acc"].at[slot])

    def y_second(step, group):
        zi, ki = where_from(step)
        r, (_, slot) = refs[group], place_of(step, group)

        @pl.when(x // 2 == ki)
        def _():
            for d in range(3):
                wait_bytes(r["rq"].at[slot, d], r["rq_sem"].at[slot, d])
                wait_bytes(r["rs"].at[slot, d], r["rs_sem"].at[slot, d])

            @pl.when(y != zi)
            def _():
                add_coded(r["acc"].at[slot], r["rq"].at[slot], r["rs"].at[slot])
                quantize(r["acc"].at[slot], r["q4"].at[slot], r["s4"].at[slot])
                for copy in y_copies(step, group):
                    copy.start()

            @pl.when(y == zi)
            def _():
                add_coded(r["acc"].at[slot], r["rq"].at[slot], r["rs"].at[slot], 1.0, r["fin"])

    def y_first(step, group):
        zi, ki = where_from(step)
        r, part = refs[group], prod.at[:, pl.ds(*GROUPS[group])]

        @pl.when(y != zi)
        def _():
            quantize(part, r["q1"].at[step], r["s1"].at[step])
            for copy in q1_copies(step, group):
                copy.start()

        @pl.when(y == zi)
        def _():
            move(part, r["acc1"].at[ki])

    def x_second(step, group):
        zi, ki = where_from(step)
        r = refs[group]

        @pl.when(y == zi)
        def _():
            for d in range(3):
                wait_bytes(r["rq1"].at[ki, d], r["rq1_sem"].at[ki, d])
                wait_bytes(r["rs1"].at[ki, d], r["rs1_sem"].at[ki, d])
            add_coded(r["acc1"].at[ki], r["rq1"].at[ki], r["rs1"].at[ki])
            for e in range(2):
                part = r["acc1"].at[ki, pl.ds(e * 128, 128), :]

                @pl.when(x != 2 * ki + e)
                def _():
                    quantize(part, r["q3"].at[ki, e], r["s3"].at[ki, e])
                    for copy in q3_copies(step, group, e):
                        copy.start()

                @pl.when(x == 2 * ki + e)
                def _():
                    move(part, r["fin"])

    def send(step, group):
        (y_first if step in Y_FIRST[group] else x_first)(step, group)

    def pass_sums(step, group):
        (x_second if step in Y_FIRST[group] else y_second)(step, group)

    def run(step, at):
        product(at, 1)
        send(step, "N")
        product(at, 0)
        send(step, "L")
        send(step, "M")

    load.wait()
    run(OWN, 0)

    @pl.when(core == 1)
    def _():
        to_second()

    for step in (A, B, PART):
        wait_bytes(tabs.at[step], t_recv.at[step])
        fetch(step).start()
    t_more = [
        remote(tabs.at[A], tabs.at[Z2], t_send.at[3], t_recv.at[Z2], first_row, col),
        remote(tabs.at[A], tabs.at[PA], t_send.at[4], t_recv.at[PA], partner, col),
        remote(tabs.at[B], tabs.at[PB], t_send.at[5], t_recv.at[PB], partner, col),
    ]
    for t in t_more:
        t.start()

    def pass_on(which, dys=DYS):
        for dy in dys:
            wait_bytes(rbuf[(A, B)[which]].at[quarter(dy)], b_recv.at[which, dy])
            d_copy(which, dy).start()
            if which == 1:
                c_copy(dy).start()

    def pass_far(dys):
        for dy in dys:
            wait_bytes(rbuf[Z2].at[quarter(dy)], c_recv.at[dy])
            d_copy(2, dy).start()

    pass_on(0, DYS[:2])
    arrived(PART, b_recv.at[2])
    for step in (A, B, PART):
        fetch(step).wait()
    build_all(PART, 1)
    run(PART, 1)
    pass_on(0, DYS[2:])
    for step in (PA, PB, Z2):
        wait_bytes(tabs.at[step], t_recv.at[step])
        fetch(step).start()
    t_last = remote(tabs.at[Z2], tabs.at[PZ2], t_send.at[6], t_recv.at[PZ2], partner, col)
    t_last.start()
    build_all(A, 0)
    run(A, 0)
    pass_sums(OWN, "N")
    for step in (PA, PB, Z2):
        fetch(step).wait()
    pass_on(1, DYS[:2])
    arrived(PA, d_recv.at[0])
    build_all(PA, 1)
    run(PA, 1)
    pass_sums(PART, "N")
    pass_on(1, DYS[2:])
    build_all(B, 0)
    run(B, 0)
    pass_sums(A, "N")
    arrived(PB, d_recv.at[1])
    build_all(PB, 1)
    run(PB, 1)
    for step in (OWN, PART, A):
        pass_sums(step, "L")
        pass_sums(step, "M")
    pass_sums(PA, "N")
    pass_far(DYS)
    wait_bytes(tabs.at[PZ2], t_recv.at[PZ2])
    fetch(PZ2).start()
    build_all(Z2, 0)
    run(Z2, 0)
    pass_sums(B, "N")
    pass_sums(B, "M")
    pass_sums(PA, "L")
    pass_sums(PA, "M")
    arrived(PZ2, d_recv.at[2])
    fetch(PZ2).wait()
    build_all(PZ2, 1)
    product(1, 1)
    send(PZ2, "N")
    pass_sums(B, "L")
    product(1, 0)
    send(PZ2, "L")
    send(PZ2, "M")
    pass_sums(PB, "N")
    pass_sums(PB, "M")
    pass_sums(Z2, "N")
    pass_sums(PB, "L")
    pass_sums(Z2, "L")
    pass_sums(Z2, "M")
    pass_sums(PZ2, "N")
    pass_sums(PZ2, "L")
    pass_sums(PZ2, "M")

    for group in ("N", "L", "M"):
        r, (start, width) = refs[group], GROUPS[group]
        for d in range(3):
            wait_bytes(r["rf"].at[d], r["rf_sem"].at[d])
            wait_bytes(r["rsf"].at[d], r["rsf_sem"].at[d])
        add_coded(r["fin"], r["rf"], r["rsf"], 0.5, out_ref.at[:, pl.ds(start, width)])

    def table_left(j, carry):
        remote(inv_ref.at[mine], tabs.at[OWN, mine], ta_send.at[j], ta_recv, row, (col + j) % 16).wait_send()
        return carry

    lax.fori_loop(1, 16, table_left, 0)
    for t in t_own + t_more + [t_last]:
        t.wait_send()
    for dy in DYS:
        for j in range(1 if dy == 0 else 0, 4):
            tile_copy(dy, j).wait_send()
        for which in range(3):
            for copy in [e_copy(j, which) for j in range(4)] if dy == 0 else [b_copies(dy, which)]:
                copy.wait_send()
        c_copy(dy).wait_send()
        for which in range(3):
            d_copy(which, dy).wait_send()
    for step in STEPS:
        zi, ki = where_from(step)
        y_groups = [g for g in GROUPS if step in Y_FIRST[g]]
        x_groups = [g for g in GROUPS if step not in Y_FIRST[g]]

        @pl.when(y != zi)
        def _():
            for group in y_groups:
                for copy in q1_copies(step, group):
                    copy.wait_send()

        for e in range(2):

            @pl.when((y == zi) & (x != 2 * ki + e))
            def _():
                for group in y_groups:
                    for copy in q3_copies(step, group, e):
                        copy.wait_send()

            @pl.when(x != 2 * ki + e)
            def _():
                for group in x_groups:
                    for copy in x_copies(step, group, e):
                        copy.wait_send()

        @pl.when((y != zi) & (x // 2 == ki))
        def _():
            for group in x_groups:
                for copy in y_copies(step, group):
                    copy.wait_send()


def ladder(buf, inv, integrals):
    ab, cd = integrals.shape
    i16, f32, bf16 = jnp.int16, jnp.float32, jnp.bfloat16
    dma = pltpu.SemaphoreType.DMA
    vmem = pltpu.VMEM
    scratch = [vmem((16 * CAP + 1, 16, 128), bf16) for _ in range(8)]
    scratch += [
        vmem((8, 16, 1, 128), jnp.int32), pltpu.SMEM((8, 16, 1, 128), jnp.int32),
        vmem((ab, cd), bf16), vmem((256, cd), bf16), vmem((256, cd), bf16), vmem((256, ab), f32),
        dma, dma((8,)), dma((4,)), dma((3, 4)),
        dma((16,)), dma, dma((7,)), dma((8,)),
        dma((16,)), dma((4,)), dma((3, 4)), dma((3, 4)), dma((4,)), dma((4,)), dma((3, 4)), dma((3, 4)),
    ]
    for group, (_, width) in GROUPS.items():
        steps, slots = (2, 1) if group == "L" else (8, 4)
        scratch += [
            vmem((steps, 2, 128, width), i16), vmem((steps, 2, 8, 128), f32),
            vmem((slots, 3, 128, width), i16), vmem((slots, 3, 8, 128), f32), vmem((slots, 128, width), f32),
            vmem((slots, 128, width), i16), vmem((slots, 8, 128), f32),
            vmem((3, 128, width), i16), vmem((3, 8, 128), f32), vmem((128, width), f32),
            dma((steps, 2)), dma((steps, 2)), dma((slots, 3)), dma((slots, 3)), dma((slots,)), dma((slots,)), dma((3,)), dma((3,)),
        ]
    for _ in "LM":
        scratch += [
            vmem((8, 256, 256), i16), vmem((8, 8, 128), f32), vmem((2, 2, 128, 256), i16), vmem((2, 2, 8, 128), f32),
            vmem((2, 3, 256, 256), i16), vmem((2, 3, 8, 128), f32), vmem((2, 256, 256), f32),
            dma((8,)), dma((8,)), dma((2, 3)), dma((2, 3)), dma((2, 2)), dma((2, 2)),
        ]
    any_space = pl.BlockSpec(memory_space=pl.ANY)
    return pl.pallas_call(
        ladder_kernel,
        out_shape=vmem((128, ab), f32),
        in_specs=[any_space, any_space, any_space],
        out_specs=pl.BlockSpec(memory_space=pltpu.VMEM),
        scratch_shapes=scratch,
        compiler_params=pltpu.CompilerParams(collective_id=0, has_side_effects=True, vmem_limit_bytes=60 << 20),
        name="ladder",
    )(buf, inv, integrals)


def shards(lam_tiles, lam_ids, integrals):
    _, s_count, pairs, tile = lam_tiles.shape
    buf, inv = bucket(lam_ids, lam_tiles.reshape(s_count, pairs, tile), lax.axis_size("col"))
    return ladder(buf, inv, integrals)


def solution(mesh):
    return jax.shard_map(
        shards,
        mesh=mesh,
        in_specs=(P(("row", "col"), None, None, None), P(("row", "col"), None), P("row", "col")),
        out_specs=P("col", "row"),
        check_vma=False,
    )
```
